32 devices in a mesh: dp: 4 (over z), ctx: 8 (over y, x, core).
Axes of the slice: x: 2, y: 2, z: 4, core: 2. Of those that a mesh axis runs over, the one named last changes fastest.
Arguments:
- queries: bfloat16 [4, 4096, 1024], P('dp', 'ctx'), may hold values from -6 to 6
- key_vectors: bfloat16 [4, 4096, 1024], P('dp', 'ctx'), may hold values from -6 to 6
- value_vectors: bfloat16 [4, 4096, 1024], P('dp', 'ctx'), may hold values from -6 to 6
- out_grad: bfloat16 [4, 4096, 1024], P('dp', 'ctx'), may hold values from -6 to 6
- column_bias: float32 [8], replicated, may hold values from -1 to 2
- column_offsets: int32 [1], replicated, may hold values from 0 to 63
Outputs:
- attended: bfloat16 [4, 4096, 1024], P('dp', 'ctx')
- query_grad: bfloat16 [4, 4096, 1024], P('dp', 'ctx')
- key_grad: bfloat16 [4, 4096, 1024], P('dp', 'ctx')
- value_grad: bfloat16 [4, 4096, 1024], P('dp', 'ctx')
- bias_grad: float32 [8], replicated
The draws below stay inside these ranges and needn't reach their ends.
All inputs are finite; a program needn't handle non-finite values.
Results may differ from the reference program's by a relative error of at most 0.005.
The reference program's roundings to bfloat16 on the way count: a program that leaves them out, or rounds other values in their place, can miss the bound.
Values may be sent and summed in bfloat16 or wider, within the bound.
A program may use at most 128 MiB of HBM per device.

```python
import jax
import jax.numpy as jnp
from jax import lax

HEADS = 8
HEAD_DIM = 128
WIDTH = 1024
LOCAL_BAND = 512
STRIDE = 4096
CB = 64
TOKENS_PER_SHARD = 512
SEQ = 4096
BATCH = 4
NCOL = 1


def draw_queries(key, part):
    values = jnp.clip(jax.random.normal(jax.random.fold_in(key, 1), (BATCH, SEQ, WIDTH), jnp.float32), -6.0, 6.0)
    return values.astype(jnp.bfloat16)


def draw_key_vectors(key, part):
    values = jnp.clip(jax.random.normal(jax.random.fold_in(key, 2), (BATCH, SEQ, WIDTH), jnp.float32), -6.0, 6.0)
    return values.astype(jnp.bfloat16)


def levels(key, shape, cuts, smallest, largest):
    gain = 1.0
    for dim, parts in cuts:
        heights = jax.random.uniform(jax.random.fold_in(jax.random.fold_in(key, 6), dim), (parts,), jnp.float32, smallest / len(cuts), largest / len(cuts))
        gain = gain * jnp.repeat(jnp.exp(heights), shape[dim] // parts).reshape((-1,) + (1,) * (len(shape) - 1 - dim))
    return gain


def scatter_about(key, shape, spread, most, shards=(), kind=jnp.bfloat16):
    gain = levels(key, shape, shards, -0.22, 0.18) if shards else 1.0
    array = jax.random.normal(key, shape, jnp.float32) * spread * gain
    return jnp.minimum(jnp.maximum(array, -most), most).astype(kind)


def setup_inputs(seed: int = 0) -> dict:
    keys = jax.random.split(jax.random.key(seed), 7)
    queries = draw_queries(jax.random.fold_in(keys[6], 71), 0)
    key_vectors = draw_key_vectors(jax.random.fold_in(keys[6], 71), 0)
    value_vectors = scatter_about(keys[2], (BATCH, SEQ, WIDTH), 1.0, 6.0, ((0, 4), (1, 8)))
    out_grad = scatter_about(keys[3], (BATCH, SEQ, WIDTH), 1.0, 6.0, ((0, 4), (1, 8)))
    column_bias = jnp.clip(jax.random.uniform(keys[4], (HEADS,), jnp.float32, -1.0, 2.0), -1.0, 2.0)
    column_offsets = jax.random.randint(keys[5], (NCOL,), 0, STRIDE // CB).astype(jnp.int32)
    return {"queries": queries, "key_vectors": key_vectors, "value_vectors": value_vectors, "out_grad": out_grad, "column_bias": column_bias, "column_offsets": column_offsets}


def column_flags(positions, offsets):
    window = positions // STRIDE
    within = positions % STRIDE
    picks = window[:, None] == jnp.arange(offsets.shape[0], dtype=jnp.int32)[None, :]
    offset_at = jnp.sum(jnp.where(picks, offsets[None, :], 0), axis=1)
    return (positions >= 0) & (within // CB == offset_at)


def head_block(qh, kb, vb, kc, vc, doh, bias_h, band_ok, band_col, col_ok):
    scale = HEAD_DIM ** -0.5
    sb = jnp.dot(qh, kb.T, preferred_element_type=jnp.float32) * scale + jnp.where(band_col, bias_h, 0.0)[None, :]
    sc = jnp.dot(qh, kc.T, preferred_element_type=jnp.float32) * scale + bias_h
    sb = jnp.where(band_ok, sb, -jnp.inf)
    sc = jnp.where(col_ok, sc, -jnp.inf)
    top = jnp.maximum(jnp.max(sb, axis=1), jnp.max(sc, axis=1))
    pb = jnp.exp(sb - top[:, None])
    pc = jnp.exp(sc - top[:, None])
    total = jnp.sum(pb, axis=1) + jnp.sum(pc, axis=1)
    wb = pb / total[:, None]
    wc = pc / total[:, None]
    wb16 = wb.astype(jnp.bfloat16)
    wc16 = wc.astype(jnp.bfloat16)
    mixed = jnp.dot(wb16, vb, preferred_element_type=jnp.float32) + jnp.dot(wc16, vc, preferred_element_type=jnp.float32)
    oh = mixed.astype(jnp.bfloat16)
    delta = jnp.sum(doh.astype(jnp.float32) * oh.astype(jnp.float32), axis=1)
    dsb = wb * (jnp.dot(doh, vb.T, preferred_element_type=jnp.float32) - delta[:, None])
    dsc = wc * (jnp.dot(doh, vc.T, preferred_element_type=jnp.float32) - delta[:, None])
    dbias = jnp.sum(jnp.where(band_col[None, :], dsb, 0.0)) + jnp.sum(dsc)
    dsb16 = dsb.astype(jnp.bfloat16)
    dsc16 = dsc.astype(jnp.bfloat16)
    dq = ((jnp.dot(dsb16, kb, preferred_element_type=jnp.float32) + jnp.dot(dsc16, kc, preferred_element_type=jnp.float32)) * scale).astype(jnp.bfloat16)
    dkb = jnp.dot(dsb16.T, qh, preferred_element_type=jnp.float32) * scale
    dvb = jnp.dot(wb16.T, doh, preferred_element_type=jnp.float32)
    dkc = jnp.dot(dsc16.T, qh, preferred_element_type=jnp.float32) * scale
    dvc = jnp.dot(wc16.T, doh, preferred_element_type=jnp.float32)
    return oh, dq, dkb, dvb, dkc, dvc, dbias


def separate_heads(x):
    return x.reshape(x.shape[0], HEADS, HEAD_DIM).transpose(1, 0, 2)


def join_heads(x):
    return x.transpose(1, 0, 2).reshape(x.shape[1], HEADS * HEAD_DIM)


def reference(queries, key_vectors, value_vectors, out_grad, column_bias, column_offsets):
    ncol = column_offsets.shape[0]
    starts = jnp.arange(ncol, dtype=jnp.int32) * STRIDE + column_offsets * CB
    colpos = jnp.repeat(starts, CB) + jnp.tile(jnp.arange(CB, dtype=jnp.int32), ncol)
    blocks = SEQ // TOKENS_PER_SHARD
    width = HEADS * HEAD_DIM
    outs_a, outs_q, outs_k, outs_v = [], [], [], []
    bias_total = jnp.zeros((HEADS,), jnp.float32)
    for sample in range(BATCH):
        qall = separate_heads(queries[sample])
        kall = key_vectors[sample]
        value_full = value_vectors[sample]
        dall = separate_heads(out_grad[sample])
        kcol = separate_heads(kall[colpos])
        vcol = separate_heads(value_full[colpos])
        padding_rows = jnp.zeros((LOCAL_BAND, width), jnp.bfloat16)
        kpad = separate_heads(jnp.concatenate([padding_rows, kall], axis=0))
        value_padded = separate_heads(jnp.concatenate([padding_rows, value_full], axis=0))

        def step(carry, index):
            dk_acc, dv_acc, dkc_acc, dvc_acc, db_acc = carry
            start_position = (index * TOKENS_PER_SHARD).astype(jnp.int32)
            qblk = lax.dynamic_slice_in_dim(qall, start_position, TOKENS_PER_SHARD, 1)
            dblk = lax.dynamic_slice_in_dim(dall, start_position, TOKENS_PER_SHARD, 1)
            kblk = lax.dynamic_slice_in_dim(kpad, start_position, LOCAL_BAND + TOKENS_PER_SHARD, 1)
            value_block = lax.dynamic_slice_in_dim(value_padded, start_position, LOCAL_BAND + TOKENS_PER_SHARD, 1)
            qpos = start_position + jnp.arange(TOKENS_PER_SHARD, dtype=jnp.int32)
            kpos = start_position - LOCAL_BAND + jnp.arange(LOCAL_BAND + TOKENS_PER_SHARD, dtype=jnp.int32)
            gap = qpos[:, None] - kpos[None, :]
            band_ok = (kpos[None, :] >= 0) & (gap >= 0) & (gap < LOCAL_BAND)
            band_col = column_flags(kpos, column_offsets)
            col_ok = colpos[None, :] <= qpos[:, None] - LOCAL_BAND

            def per_head(items):
                return head_block(items[0], items[1], items[2], items[3], items[4], items[5], items[6], band_ok, band_col, col_ok)

            oh, dq, dkb, dvb, dkc, dvc, dbias = lax.map(per_head, (qblk, kblk, value_block, kcol, vcol, dblk, column_bias))
            cur_k = lax.dynamic_slice_in_dim(dk_acc, start_position, LOCAL_BAND + TOKENS_PER_SHARD, 1)
            cur_v = lax.dynamic_slice_in_dim(dv_acc, start_position, LOCAL_BAND + TOKENS_PER_SHARD, 1)
            dk_acc = lax.dynamic_update_slice_in_dim(dk_acc, cur_k + dkb, start_position, 1)
            dv_acc = lax.dynamic_update_slice_in_dim(dv_acc, cur_v + dvb, start_position, 1)
            return (dk_acc, dv_acc, dkc_acc + dkc, dvc_acc + dvc, db_acc + dbias), (oh, dq)

        init = (jnp.zeros((HEADS, LOCAL_BAND + SEQ, HEAD_DIM), jnp.float32), jnp.zeros((HEADS, LOCAL_BAND + SEQ, HEAD_DIM), jnp.float32),
                jnp.zeros((HEADS, ncol * CB, HEAD_DIM), jnp.float32), jnp.zeros((HEADS, ncol * CB, HEAD_DIM), jnp.float32),
                jnp.zeros((HEADS,), jnp.float32))
        carry, ys = lax.scan(step, init, jnp.arange(blocks, dtype=jnp.int32))
        dk_acc, dv_acc, dkc_acc, dvc_acc, db_acc = carry
        attended = ys[0].transpose(0, 2, 1, 3).reshape(SEQ, width)
        qgrad = ys[1].transpose(0, 2, 1, 3).reshape(SEQ, width)
        kgrad = join_heads(dk_acc[:, LOCAL_BAND:]).at[colpos].add(join_heads(dkc_acc))
        vgrad = join_heads(dv_acc[:, LOCAL_BAND:]).at[colpos].add(join_heads(dvc_acc))
        outs_a.append(attended)
        outs_q.append(qgrad)
        outs_k.append(kgrad.astype(jnp.bfloat16))
        outs_v.append(vgrad.astype(jnp.bfloat16))
        bias_total = bias_total + db_acc
    return (jnp.stack(outs_a), jnp.stack(outs_q), jnp.stack(outs_k), jnp.stack(outs_v), bias_total)
```

```python
import functools

import jax
import jax.numpy as jnp
from jax import lax
from jax.experimental import pallas as pl
from jax.experimental.pallas import tpu as pltpu
from jax.sharding import PartitionSpec as P

HEADS = 8
HEAD_DIM = 128
LOCAL_BAND = 512
STRIDE = 4096
CB = 64
TOKENS_PER_SHARD = 512


def from_behind(value, axis, by):
    size = lax.axis_size(axis)
    pairs = [(i, i + by) for i in range(size) if 0 <= i + by < size]
    return lax.ppermute(value, axis, pairs)


def column_flags(positions, offsets):
    window = positions // STRIDE
    within = positions % STRIDE
    picks = window[:, None] == jnp.arange(offsets.shape[0], dtype=jnp.int32)[None, :]
    offset_at = jnp.sum(jnp.where(picks, offsets[None, :], 0), axis=1)
    return (positions >= 0) & (within // CB == offset_at)


def head_block(qh, kb, vb, kc, vc, doh, bias_h, band_ok, band_col, col_ok):
    scale = HEAD_DIM ** (-0.5)
    sb = (
        jnp.dot(qh, kb.T, preferred_element_type=jnp.float32) * scale
        + jnp.where(band_col, bias_h, 0.0)[None, :]
    )
    sc = jnp.dot(qh, kc.T, preferred_element_type=jnp.float32) * scale + bias_h
    sb = jnp.where(band_ok, sb, -jnp.inf)
    sc = jnp.where(col_ok, sc, -jnp.inf)
    top = jnp.maximum(jnp.max(sb, axis=1), jnp.max(sc, axis=1))
    pb = jnp.exp(sb - top[:, None])
    pc = jnp.exp(sc - top[:, None])
    total = jnp.sum(pb, axis=1) + jnp.sum(pc, axis=1)
    wb = pb / total[:, None]
    wc = pc / total[:, None]
    wb16 = wb.astype(jnp.bfloat16)
    wc16 = wc.astype(jnp.bfloat16)
    mixed = jnp.dot(wb16, vb, preferred_element_type=jnp.float32) + jnp.dot(
        wc16, vc, preferred_element_type=jnp.float32
    )
    oh = mixed.astype(jnp.bfloat16)
    delta = jnp.sum(doh.astype(jnp.float32) * oh.astype(jnp.float32), axis=1)
    dsb = wb * (jnp.dot(doh, vb.T, preferred_element_type=jnp.float32) - delta[:, None])
    dsc = wc * (jnp.dot(doh, vc.T, preferred_element_type=jnp.float32) - delta[:, None])
    dbias = jnp.sum(jnp.where(band_col[None, :], dsb, 0.0)) + jnp.sum(dsc)
    dsb16 = dsb.astype(jnp.bfloat16)
    dsc16 = dsc.astype(jnp.bfloat16)
    dq = (
        (
            jnp.dot(dsb16, kb, preferred_element_type=jnp.float32)
            + jnp.dot(dsc16, kc, preferred_element_type=jnp.float32)
        )
        * scale
    ).astype(jnp.bfloat16)
    dkb = jnp.dot(dsb16.T, qh, preferred_element_type=jnp.float32) * scale
    dvb = jnp.dot(wb16.T, doh, preferred_element_type=jnp.float32)
    dkc = jnp.dot(dsc16.T, qh, preferred_element_type=jnp.float32) * scale
    dvc = jnp.dot(wc16.T, doh, preferred_element_type=jnp.float32)
    return (oh, dq, dkb, dvb, dkc, dvc, dbias, top, total, delta)


def separate_heads(x):
    return x.reshape(x.shape[0], HEADS, HEAD_DIM).transpose(1, 0, 2)


def join_heads(x):
    return x.transpose(1, 0, 2).reshape(x.shape[1], HEADS * HEAD_DIM)


def per_device_many_windows(queries, key_vectors, value_vectors, out_grad, column_bias, column_offsets):
    here = lax.axis_index("ctx")
    count = lax.axis_size("ctx")
    start_position = here * TOKENS_PER_SHARD
    width = queries.shape[2]
    query_rows = queries[0]
    key_rows = key_vectors[0]
    value_rows = value_vectors[0]
    grad_rows = out_grad[0]
    ncol = column_offsets.shape[0]
    block_starts = jnp.arange(ncol, dtype=jnp.int32) * STRIDE + column_offsets * CB
    colpos = jnp.repeat(block_starts, CB) + jnp.tile(jnp.arange(CB, dtype=jnp.int32), ncol)
    window = start_position // STRIDE
    own_start = window * STRIDE + column_offsets[window] * CB
    local = jnp.clip(own_start - start_position, 0, TOKENS_PER_SHARD - CB)
    piece_k = lax.dynamic_slice_in_dim(key_rows, local, CB, 0)
    piece_v = lax.dynamic_slice_in_dim(value_rows, local, CB, 0)
    pieces_k, pieces_v = (
        lax.all_gather(piece_k, "ctx", axis=0, tiled=True),
        lax.all_gather(piece_v, "ctx", axis=0, tiled=True),
    )
    owner = block_starts // TOKENS_PER_SHARD
    col_k = pieces_k.reshape(count, CB, width)[owner].reshape(ncol * CB, width)
    col_v = pieces_v.reshape(count, CB, width)[owner].reshape(ncol * CB, width)
    prev_k, prev_v = from_behind((key_rows, value_rows), "ctx", 1)
    band_k = jnp.concatenate([prev_k, key_rows], axis=0)
    band_v = jnp.concatenate([prev_v, value_rows], axis=0)
    qpos = start_position + jnp.arange(TOKENS_PER_SHARD, dtype=jnp.int32)
    kpos = start_position - LOCAL_BAND + jnp.arange(LOCAL_BAND + TOKENS_PER_SHARD, dtype=jnp.int32)
    gap = qpos[:, None] - kpos[None, :]
    band_ok = (kpos[None, :] >= 0) & (gap >= 0) & (gap < LOCAL_BAND)
    band_col = column_flags(kpos, column_offsets)
    col_ok = colpos[None, :] <= qpos[:, None] - LOCAL_BAND

    def per_head(items):
        return head_block(
            items[0],
            items[1],
            items[2],
            items[3],
            items[4],
            items[5],
            items[6],
            band_ok,
            band_col,
            col_ok,
        )

    results = lax.map(
        per_head,
        (
            separate_heads(query_rows),
            separate_heads(band_k),
            separate_heads(band_v),
            separate_heads(col_k),
            separate_heads(col_v),
            separate_heads(grad_rows),
            column_bias,
        ),
    )
    oh, dq, dkb, dvb, dkc, dvc, dbias, top, total, delta = results
    attended = join_heads(oh)
    query_grad = join_heads(dq)
    dk_band = join_heads(dkb)
    dv_band = join_heads(dvb)
    own_dk = dk_band[dk_band.shape[0] - TOKENS_PER_SHARD :]
    own_dv = dv_band[dv_band.shape[0] - TOKENS_PER_SHARD :]
    back_k, back_v = from_behind((dk_band[:LOCAL_BAND], dv_band[:LOCAL_BAND]), "ctx", -1)
    own_dk = own_dk.at[TOKENS_PER_SHARD - LOCAL_BAND :].add(back_k)
    own_dv = own_dv.at[TOKENS_PER_SHARD - LOCAL_BAND :].add(back_v)
    summed_k, summed_v = lax.psum((join_heads(dkc), join_heads(dvc)), "ctx")
    flags = column_flags(qpos, column_offsets)
    source = jnp.clip(qpos // STRIDE * CB + qpos % CB, 0, ncol * CB - 1)
    own_dk = own_dk + jnp.where(flags[:, None], summed_k[source], 0.0)
    own_dv = own_dv + jnp.where(flags[:, None], summed_v[source], 0.0)
    bias_grad = lax.psum(dbias, ("dp", "ctx"))
    return (
        attended[None],
        query_grad[None],
        own_dk.astype(jnp.bfloat16)[None],
        own_dv.astype(jnp.bfloat16)[None],
        bias_grad,
    )


LOG2E = 1.4426950408889634
SCALE = HEAD_DIM ** (-0.5)
NEG = -1e30
HALF = 256
T = TOKENS_PER_SHARD
D = HEAD_DIM
MESH = pl.DeviceIdType.MESH
NT = (((1,), (1,)), ((), ()))
TN = (((0,), (0,)), ((), ()))


def dot_nt(a, b):
    return lax.dot_general(a, b, NT, preferred_element_type=jnp.float32)


def dot_tn(a, b):
    return lax.dot_general(a, b, TN, preferred_element_type=jnp.float32)


def dot_nn(a, b):
    return jnp.dot(a, b, preferred_element_type=jnp.float32)


def flip(index, step):
    return index + step * (1 - 2 * ((index // step) % 2))


def fold(x):
    return x[:, :128] + x[:, 128:]


def fused_kernel(
    n,
    ndp,
    offs_ref,
    bias_ref,
    q_ref,
    k_ref,
    v_ref,
    g_ref,
    o_ref,
    dq_ref,
    dk_ref,
    dv_ref,
    db_ref,
    prev,
    back,
    out,
    own,
    col,
    colr,
    acc,
    accr,
    bacc,
    baccr,
    flag,
    masks,
    halo_s,
    halo_r,
    ret_s,
    ret_r,
    cg_s,
    cg_r,
    red_s,
    red_r,
    b_s,
    b_r,
):
    me = lax.axis_index("ctx")
    mine = lax.axis_index("dp")
    steps = []
    while 2 ** len(steps) < n:
        steps.append(2 ** len(steps))
    dsteps = []
    while 2 ** len(dsteps) < ndp:
        dsteps.append(2 ** len(dsteps))
    S = len(steps)
    start = me * T
    col_row = offs_ref[0:1, :]
    col_start = col_row[:, 0:128]
    col_start2 = col_row[:, 0:HALF]

    other = me + 2 * (me % 2) - 1
    has_other = (other >= 0) & (other < n)
    barrier = pltpu.get_barrier_semaphore()
    for st in steps:
        pl.semaphore_signal(barrier, inc=1, device_id={"ctx": flip(me, st)}, device_id_type=MESH)
    for st in dsteps:
        pl.semaphore_signal(barrier, inc=1, device_id={"dp": flip(mine, st)}, device_id_type=MESH)

    @pl.when(has_other)
    def _():
        pl.semaphore_signal(barrier, inc=1, device_id={"ctx": other}, device_id_type=MESH)

    for i, ref in ((0, k_ref), (1, v_ref)):
        block = jnp.zeros((CB, ref.shape[1]), jnp.float32)
        for r in range(T // CB):
            held = (col_row == start + r * CB).astype(jnp.float32)
            block = block + ref[r * CB : (r + 1) * CB, :].astype(jnp.float32) * held
        col[i * CB : (i + 1) * CB, :] = block.astype(jnp.bfloat16)

    row = lax.broadcasted_iota(jnp.int32, (HALF, HALF), 0)
    lane = lax.broadcasted_iota(jnp.int32, (HALF, HALF), 1)
    masks[0] = jnp.where(row > lane, 0.0, NEG)
    masks[1] = jnp.where(row <= lane, 0.0, NEG)
    kpos = start - T + lax.broadcasted_iota(jnp.int32, (2 * T, 128), 0)
    flag[...] = ((kpos >= col_start) & (kpos < col_start + CB)).astype(jnp.float32)

    @pl.when(me == 0)
    def _():
        prev[...] = jnp.zeros_like(prev)

    @pl.when(me == n - 1)
    def _():
        back[...] = jnp.zeros_like(back)

    @pl.when(has_other)
    def _():
        pl.semaphore_wait(barrier, S + len(dsteps) + 1)

    @pl.when((other < 0) | (other >= n))
    def _():
        pl.semaphore_wait(barrier, S + len(dsteps))

    def gather_step(s):
        return pltpu.make_async_remote_copy(
            src_ref=col,
            dst_ref=colr.at[s],
            send_sem=cg_s.at[s],
            recv_sem=cg_r.at[s],
            device_id={"ctx": flip(me, steps[s])},
            device_id_type=MESH,
        )

    def halo(i, h):
        c = pl.ds(pl.multiple_of(h * D, D), D)
        return pltpu.make_async_remote_copy(
            src_ref=(k_ref, v_ref)[i].at[:, c],
            dst_ref=prev.at[i, :, c],
            send_sem=halo_s.at[i, h],
            recv_sem=halo_r.at[i, h],
            device_id={"ctx": me + 1},
            device_id_type=MESH,
        )

    def give_back(i, h):
        c = pl.ds(pl.multiple_of(h * D, D), D)
        return pltpu.make_async_remote_copy(
            src_ref=out.at[i, :, c],
            dst_ref=back.at[i, :, c],
            send_sem=ret_s.at[i, h],
            recv_sem=ret_r.at[i, h],
            device_id={"ctx": me - 1},
            device_id_type=MESH,
        )

    def reduce_step(s, h):
        return pltpu.make_async_remote_copy(
            src_ref=acc.at[h],
            dst_ref=accr.at[s, h],
            send_sem=red_s.at[s, h],
            recv_sem=red_r.at[s, h],
            device_id={"ctx": flip(me, steps[s])},
            device_id_type=MESH,
        )

    def send_halo():
        @pl.when(me < n - 1)
        def _():
            @pl.loop(0, HEADS)
            def _(h):
                halo(0, h).start()
                halo(1, h).start()

    for s in range(S):
        gather_step(s).start()
        if s == S - 1:
            send_halo()
        gather_step(s).wait()
        col[...] = col[...] + colr[s]

    def compute(h):
        @pl.when(me > 0)
        def _():
            halo(0, h).wait_recv()
            halo(1, h).wait_recv()

        c = pl.ds(pl.multiple_of(h * D, D), D)
        bias2 = bias_ref[pl.ds(h, 1), :] * LOG2E
        outside = jnp.where(me == 0, NEG, 0.0)
        kc = col[0:CB, c]
        vc = col[CB : 2 * CB, c]
        keys = [prev[0, 0:HALF, c], prev[0, HALF:T, c], k_ref[0:HALF, c], k_ref[HALF:T, c]]
        vals = [prev[1, 0:HALF, c], prev[1, HALF:T, c], v_ref[0:HALF, c], v_ref[HALF:T, c]]
        dks = [None] * 4
        dvs = [None] * 4
        dkc = dvc = None
        dbv = jnp.zeros((1, 128), jnp.float32)
        for b in range(2):
            rows = slice(b * HALF, (b + 1) * HALF)
            qb = q_ref[rows, c]
            gb = g_ref[rows, c]
            scores = []
            for p in range(3):
                j = b + p
                kb = flag[j * HALF : (j + 1) * HALF, :] * bias2
                if j < 2:
                    kb = kb + outside
                s = dot_nt(keys[j], qb) * (SCALE * LOG2E) + jnp.concatenate([kb, kb], axis=1)
                if p == 0:
                    s = s + masks[0]
                if p == 2:
                    s = s + masks[1]
                scores.append(s)
            cpos = col_start2 + lax.broadcasted_iota(jnp.int32, (CB, HALF), 0)
            qpos = start + b * HALF + lax.broadcasted_iota(jnp.int32, (CB, HALF), 1)
            sc = dot_nt(kc, qb) * (SCALE * LOG2E) + jnp.concatenate([bias2, bias2], axis=1)
            scores.append(jnp.where(cpos <= qpos - LOCAL_BAND, sc, NEG))
            top = functools.reduce(
                jnp.maximum, [jnp.max(s, axis=0, keepdims=True) for s in scores]
            )
            ps = [jnp.exp2(s - top) for s in scores]
            total = functools.reduce(jnp.add, [jnp.sum(p, axis=0, keepdims=True) for p in ps])
            inv = 1.0 / total
            ws = [p * inv for p in ps]
            w16 = [w.astype(jnp.bfloat16) for w in ws]
            vb = [vals[b], vals[b + 1], vals[b + 2], vc]
            kb = [keys[b], keys[b + 1], keys[b + 2], kc]
            ot = functools.reduce(jnp.add, [dot_tn(v, w) for v, w in zip(vb, w16)])
            ot = ot.astype(jnp.bfloat16).astype(jnp.float32)
            o_ref[rows, c] = ot.T.astype(jnp.bfloat16)
            delta = jnp.sum(gb.astype(jnp.float32).T * ot, axis=0, keepdims=True)
            ds = [w * (dot_nt(v, gb) - delta) for v, w in zip(vb, ws)]
            for p in range(3):
                j = b + p
                f = flag[j * HALF : (j + 1) * HALF, :]
                dbv = dbv + jnp.sum(fold(ds[p]) * f, axis=0, keepdims=True)
            dbv = dbv + jnp.sum(fold(ds[3]), axis=0, keepdims=True)
            ds16 = [d.astype(jnp.bfloat16) for d in ds]
            dqt = functools.reduce(jnp.add, [dot_tn(k, d) for k, d in zip(kb, ds16)])
            dq_ref[rows, c] = (dqt * SCALE).T.astype(jnp.bfloat16)
            for p in range(3):
                j = b + p
                dv = dot_nn(w16[p], gb)
                dk = dot_nn(ds16[p], qb)
                dvs[j] = dv if dvs[j] is None else dvs[j] + dv
                dks[j] = dk if dks[j] is None else dks[j] + dk
            dv = dot_nn(w16[3], gb)
            dk = dot_nn(ds16[3], qb)
            dvc = dv if dvc is None else dvc + dv
            dkc = dk if dkc is None else dkc + dk
        for j in range(2):
            rows = slice(j * HALF, (j + 1) * HALF)
            out[0, rows, c] = (dks[j] * SCALE).astype(jnp.bfloat16)
            out[1, rows, c] = dvs[j].astype(jnp.bfloat16)
            own[0, rows, c] = dks[j + 2] * SCALE
            own[1, rows, c] = dvs[j + 2]
        acc[h, 0:CB, :] = dkc * SCALE
        acc[h, CB : 2 * CB, :] = dvc
        acc[h, 2 * CB :, :] = jnp.broadcast_to(dbv, (8, 128))

        @pl.when(me > 0)
        def _():
            give_back(0, h).start()
            give_back(1, h).start()

    def finish(h):
        @pl.when(me < n - 1)
        def _():
            give_back(0, h).wait_recv()
            give_back(1, h).wait_recv()

        c = pl.ds(pl.multiple_of(h * D, D), D)
        for i, ref in ((0, dk_ref), (1, dv_ref)):
            summed = acc[h, i * CB : (i + 1) * CB, :]
            for r in range(T // CB):
                rows = slice(r * CB, (r + 1) * CB)
                held = (col_start == start + r * CB).astype(jnp.float32)
                grad = own[i, rows, c] + back[i, rows, c].astype(jnp.float32) + summed * held
                ref[rows, c] = grad.astype(jnp.bfloat16)

    def turn(t, carry):
        @pl.when(t < HEADS)
        def _():
            compute(t)

        for s in range(S + 1):
            h = t - s

            @pl.when((h >= 0) & (h < HEADS))
            def _():
                if s > 0:
                    reduce_step(s - 1, h).wait()
                    acc[h] = acc[h] + accr[s - 1, h]
                if s < S:
                    reduce_step(s, h).start()
                else:
                    finish(h)

        return carry

    lax.fori_loop(0, HEADS + S, turn, 0)

    for h in range(HEADS):
        bacc[h : h + 1, :] = acc[h, 2 * CB : 2 * CB + 1, :]
    for s in range(len(dsteps)):
        copy = pltpu.make_async_remote_copy(
            src_ref=bacc,
            dst_ref=baccr.at[s],
            send_sem=b_s.at[s],
            recv_sem=b_r.at[s],
            device_id={"dp": flip(mine, dsteps[s])},
            device_id_type=MESH,
        )
        copy.start()
        copy.wait()
        bacc[...] = bacc[...] + baccr[s]
    db_ref[...] = bacc[...]

    @pl.when(me < n - 1)
    def _():
        @pl.loop(0, HEADS)
        def _(h):
            halo(0, h).wait_send()
            halo(1, h).wait_send()

    @pl.when(me > 0)
    def _():
        @pl.loop(0, HEADS)
        def _(h):
            give_back(0, h).wait_send()
            give_back(1, h).wait_send()


def per_device(queries, key_vectors, value_vectors, out_grad, column_bias, column_offsets):
    if column_offsets.shape[0] > 1:
        return per_device_many_windows(
            queries, key_vectors, value_vectors, out_grad, column_bias, column_offsets
        )
    n = lax.axis_size("ctx")
    ndp = lax.axis_size("dp")
    S = n.bit_length() - 1
    SD = ndp.bit_length() - 1
    width = queries.shape[2]
    vmem = pl.BlockSpec(memory_space=pltpu.VMEM)
    wide = jax.ShapeDtypeStruct((T, width), jnp.bfloat16)
    o, dq, dk, dv, db = pl.pallas_call(
        functools.partial(fused_kernel, n, ndp),
        out_shape=(wide, wide, wide, wide, jax.ShapeDtypeStruct((HEADS, 128), jnp.float32)),
        in_specs=[vmem, vmem, vmem, vmem, vmem, vmem],
        out_specs=(vmem, vmem, vmem, vmem, vmem),
        scratch_shapes=[
            pltpu.VMEM((2, T, width), jnp.bfloat16),
            pltpu.VMEM((2, T, width), jnp.bfloat16),
            pltpu.VMEM((2, T, width), jnp.bfloat16),
            pltpu.VMEM((2, T, width), jnp.float32),
            pltpu.VMEM((2 * CB, width), jnp.bfloat16),
            pltpu.VMEM((S, 2 * CB, width), jnp.bfloat16),
            pltpu.VMEM((HEADS, 2 * CB + 8, 128), jnp.float32),
            pltpu.VMEM((S, HEADS, 2 * CB + 8, 128), jnp.float32),
            pltpu.VMEM((HEADS, 128), jnp.float32),
            pltpu.VMEM((SD, HEADS, 128), jnp.float32),
            pltpu.VMEM((2 * T, 128), jnp.float32),
            pltpu.VMEM((2, HALF, HALF), jnp.float32),
            pltpu.SemaphoreType.DMA((2, HEADS)),
            pltpu.SemaphoreType.DMA((2, HEADS)),
            pltpu.SemaphoreType.DMA((2, HEADS)),
            pltpu.SemaphoreType.DMA((2, HEADS)),
            pltpu.SemaphoreType.DMA((S,)),
            pltpu.SemaphoreType.DMA((S,)),
            pltpu.SemaphoreType.DMA((S, HEADS)),
            pltpu.SemaphoreType.DMA((S, HEADS)),
            pltpu.SemaphoreType.DMA((SD,)),
            pltpu.SemaphoreType.DMA((SD,)),
        ],
        compiler_params=pltpu.CompilerParams(
            collective_id=0, has_side_effects=True, vmem_limit_bytes=56 * 2**20
        ),
    )(
        jnp.broadcast_to(column_offsets[:, None] * CB, (8, width)),
        jnp.broadcast_to(column_bias[:, None], (HEADS, 128)),
        queries[0],
        key_vectors[0],
        value_vectors[0],
        out_grad[0],
    )
    return o[None], dq[None], dk[None], dv[None], jnp.sum(db, axis=1)


def solution(mesh):
    placed = (
        P("dp", "ctx", None),
        P("dp", "ctx", None),
        P("dp", "ctx", None),
        P("dp", "ctx", None),
        P(),
        P(),
    )
    return jax.shard_map(
        per_device,
        mesh=mesh,
        in_specs=placed,
        out_specs=(
            P("dp", "ctx", None),
            P("dp", "ctx", None),
            P("dp", "ctx", None),
            P("dp", "ctx", None),
            P(),
        ),
        check_vma=False,
    )
```

```python
import functools

import jax
import jax.numpy as jnp
from jax import lax
from jax.experimental import pallas as pl
from jax.experimental.pallas import tpu as pltpu
from jax.sharding import PartitionSpec as P

HEADS = 8
HEAD_DIM = 128
LOCAL_BAND = 512
STRIDE = 4096
CB = 64
TOKENS_PER_SHARD = 512


def from_behind(value, axis, by):
    size = lax.axis_size(axis)
    pairs = [(i, i + by) for i in range(size) if 0 <= i + by < size]
    return lax.ppermute(value, axis, pairs)


def column_flags(positions, offsets):
    window = positions // STRIDE
    within = positions % STRIDE
    picks = window[:, None] == jnp.arange(offsets.shape[0], dtype=jnp.int32)[None, :]
    offset_at = jnp.sum(jnp.where(picks, offsets[None, :], 0), axis=1)
    return (positions >= 0) & (within // CB == offset_at)


def head_block(qh, kb, vb, kc, vc, doh, bias_h, band_ok, band_col, col_ok):
    scale = HEAD_DIM ** (-0.5)
    sb = (
        jnp.dot(qh, kb.T, preferred_element_type=jnp.float32) * scale
        + jnp.where(band_col, bias_h, 0.0)[None, :]
    )
    sc = jnp.dot(qh, kc.T, preferred_element_type=jnp.float32) * scale + bias_h
    sb = jnp.where(band_ok, sb, -jnp.inf)
    sc = jnp.where(col_ok, sc, -jnp.inf)
    top = jnp.maximum(jnp.max(sb, axis=1), jnp.max(sc, axis=1))
    pb = jnp.exp(sb - top[:, None])
    pc = jnp.exp(sc - top[:, None])
    total = jnp.sum(pb, axis=1) + jnp.sum(pc, axis=1)
    wb = pb / total[:, None]
    wc = pc / total[:, None]
    wb16 = wb.astype(jnp.bfloat16)
    wc16 = wc.astype(jnp.bfloat16)
    mixed = jnp.dot(wb16, vb, preferred_element_type=jnp.float32) + jnp.dot(
        wc16, vc, preferred_element_type=jnp.float32
    )
    oh = mixed.astype(jnp.bfloat16)
    delta = jnp.sum(doh.astype(jnp.float32) * oh.astype(jnp.float32), axis=1)
    dsb = wb * (jnp.dot(doh, vb.T, preferred_element_type=jnp.float32) - delta[:, None])
    dsc = wc * (jnp.dot(doh, vc.T, preferred_element_type=jnp.float32) - delta[:, None])
    dbias = jnp.sum(jnp.where(band_col[None, :], dsb, 0.0)) + jnp.sum(dsc)
    dsb16 = dsb.astype(jnp.bfloat16)
    dsc16 = dsc.astype(jnp.bfloat16)
    dq = (
        (
            jnp.dot(dsb16, kb, preferred_element_type=jnp.float32)
            + jnp.dot(dsc16, kc, preferred_element_type=jnp.float32)
        )
        * scale
    ).astype(jnp.bfloat16)
    dkb = jnp.dot(dsb16.T, qh, preferred_element_type=jnp.float32) * scale
    dvb = jnp.dot(wb16.T, doh, preferred_element_type=jnp.float32)
    dkc = jnp.dot(dsc16.T, qh, preferred_element_type=jnp.float32) * scale
    dvc = jnp.dot(wc16.T, doh, preferred_element_type=jnp.float32)
    return (oh, dq, dkb, dvb, dkc, dvc, dbias, top, total, delta)


def separate_heads(x):
    return x.reshape(x.shape[0], HEADS, HEAD_DIM).transpose(1, 0, 2)


def join_heads(x):
    return x.transpose(1, 0, 2).reshape(x.shape[1], HEADS * HEAD_DIM)


def per_device_many_windows(queries, key_vectors, value_vectors, out_grad, column_bias, column_offsets):
    here = lax.axis_index("ctx")
    count = lax.axis_size("ctx")
    start_position = here * TOKENS_PER_SHARD
    width = queries.shape[2]
    query_rows = queries[0]
    key_rows = key_vectors[0]
    value_rows = value_vectors[0]
    grad_rows = out_grad[0]
    ncol = column_offsets.shape[0]
    block_starts = jnp.arange(ncol, dtype=jnp.int32) * STRIDE + column_offsets * CB
    colpos = jnp.repeat(block_starts, CB) + jnp.tile(jnp.arange(CB, dtype=jnp.int32), ncol)
    window = start_position // STRIDE
    own_start = window * STRIDE + column_offsets[window] * CB
    local = jnp.clip(own_start - start_position, 0, TOKENS_PER_SHARD - CB)
    piece_k = lax.dynamic_slice_in_dim(key_rows, local, CB, 0)
    piece_v = lax.dynamic_slice_in_dim(value_rows, local, CB, 0)
    pieces_k, pieces_v = (
        lax.all_gather(piece_k, "ctx", axis=0, tiled=True),
        lax.all_gather(piece_v, "ctx", axis=0, tiled=True),
    )
    owner = block_starts // TOKENS_PER_SHARD
    col_k = pieces_k.reshape(count, CB, width)[owner].reshape(ncol * CB, width)
    col_v = pieces_v.reshape(count, CB, width)[owner].reshape(ncol * CB, width)
    prev_k, prev_v = from_behind((key_rows, value_rows), "ctx", 1)
    band_k = jnp.concatenate([prev_k, key_rows], axis=0)
    band_v = jnp.concatenate([prev_v, value_rows], axis=0)
    qpos = start_position + jnp.arange(TOKENS_PER_SHARD, dtype=jnp.int32)
    kpos = start_position - LOCAL_BAND + jnp.arange(LOCAL_BAND + TOKENS_PER_SHARD, dtype=jnp.int32)
    gap = qpos[:, None] - kpos[None, :]
    band_ok = (kpos[None, :] >= 0) & (gap >= 0) & (gap < LOCAL_BAND)
    band_col = column_flags(kpos, column_offsets)
    col_ok = colpos[None, :] <= qpos[:, None] - LOCAL_BAND

    def per_head(items):
        return head_block(
            items[0],
            items[1],
            items[2],
            items[3],
            items[4],
            items[5],
            items[6],
            band_ok,
            band_col,
            col_ok,
        )

    results = lax.map(
        per_head,
        (
            separate_heads(query_rows),
            separate_heads(band_k),
            separate_heads(band_v),
            separate_heads(col_k),
            separate_heads(col_v),
            separate_heads(grad_rows),
            column_bias,
        ),
    )
    oh, dq, dkb, dvb, dkc, dvc, dbias, top, total, delta = results
    attended = join_heads(oh)
    query_grad = join_heads(dq)
    dk_band = join_heads(dkb)
    dv_band = join_heads(dvb)
    own_dk = dk_band[dk_band.shape[0] - TOKENS_PER_SHARD :]
    own_dv = dv_band[dv_band.shape[0] - TOKENS_PER_SHARD :]
    back_k, back_v = from_behind((dk_band[:LOCAL_BAND], dv_band[:LOCAL_BAND]), "ctx", -1)
    own_dk = own_dk.at[TOKENS_PER_SHARD - LOCAL_BAND :].add(back_k)
    own_dv = own_dv.at[TOKENS_PER_SHARD - LOCAL_BAND :].add(back_v)
    summed_k, summed_v = lax.psum((join_heads(dkc), join_heads(dvc)), "ctx")
    flags = column_flags(qpos, column_offsets)
    source = jnp.clip(qpos // STRIDE * CB + qpos % CB, 0, ncol * CB - 1)
    own_dk = own_dk + jnp.where(flags[:, None], summed_k[source], 0.0)
    own_dv = own_dv + jnp.where(flags[:, None], summed_v[source], 0.0)
    bias_grad = lax.psum(dbias, ("dp", "ctx"))
    return (
        attended[None],
        query_grad[None],
        own_dk.astype(jnp.bfloat16)[None],
        own_dv.astype(jnp.bfloat16)[None],
        bias_grad,
    )


LOG2E = 1.4426950408889634
SCALE = HEAD_DIM ** (-0.5)
NEG = -1e30
HALF = 256
T = TOKENS_PER_SHARD
D = HEAD_DIM
MESH = pl.DeviceIdType.MESH
NT = (((1,), (1,)), ((), ()))
TN = (((0,), (0,)), ((), ()))


def dot_nt(a, b):
    return lax.dot_general(a, b, NT, preferred_element_type=jnp.float32)


def dot_tn(a, b):
    return lax.dot_general(a, b, TN, preferred_element_type=jnp.float32)


def dot_nn(a, b):
    return jnp.dot(a, b, preferred_element_type=jnp.float32)


def flip(index, step):
    return index + step * (1 - 2 * ((index // step) % 2))


def fold(x):
    return x[:, :128] + x[:, 128:]


def fused_kernel(
    n,
    ndp,
    offs_ref,
    bias_ref,
    q_ref,
    k_ref,
    v_ref,
    g_ref,
    o_ref,
    dq_ref,
    dk_ref,
    dv_ref,
    db_ref,
    prev,
    back,
    out,
    own,
    col,
    colr,
    acc,
    accr,
    bacc,
    baccr,
    flag,
    masks,
    relay,
    rel_s,
    rel_r,
    halo_s,
    halo_r,
    ret_s,
    ret_r,
    cg_s,
    cg_r,
    red_s,
    red_r,
    b_s,
    b_r,
):
    me = lax.axis_index("ctx")
    mine = lax.axis_index("dp")
    steps = []
    while 2 ** len(steps) < n:
        steps.append(2 ** len(steps))
    dsteps = []
    while 2 ** len(dsteps) < ndp:
        dsteps.append(2 ** len(dsteps))
    S = len(steps)
    start = me * T
    col_row = offs_ref[0:1, :]
    col_start = col_row[:, 0:128]
    col_start2 = col_row[:, 0:HALF]

    even = me % 2 == 0
    mid = n // 2
    relayed = n == 8
    other = me + 2 * (me % 2) - 1
    has_other = (other >= 0) & (other < n)
    ends = (me == 0) | (me == n - 1)
    middle = (me == mid - 1) | (me == mid)
    barrier = pltpu.get_barrier_semaphore()
    for st in steps:
        pl.semaphore_signal(barrier, inc=1, device_id={"ctx": flip(me, st)}, device_id_type=MESH)
    for st in dsteps:
        pl.semaphore_signal(barrier, inc=1, device_id={"dp": flip(mine, st)}, device_id_type=MESH)

    @pl.when(has_other)
    def _():
        pl.semaphore_signal(barrier, inc=1, device_id={"ctx": other}, device_id_type=MESH)

    if relayed:

        @pl.when(ends | middle)
        def _():
            pl.semaphore_signal(barrier, inc=1, device_id={"ctx": flip(flip(me, 1), 2)}, device_id_type=MESH)

    for i, ref in ((0, k_ref), (1, v_ref)):
        block = jnp.zeros((CB, ref.shape[1]), jnp.float32)
        for r in range(T // CB):
            held = (col_row == start + r * CB).astype(jnp.float32)
            block = block + ref[r * CB : (r + 1) * CB, :].astype(jnp.float32) * held
        col[i * CB : (i + 1) * CB, :] = block.astype(jnp.bfloat16)

    row = lax.broadcasted_iota(jnp.int32, (HALF, HALF), 0)
    lane = lax.broadcasted_iota(jnp.int32, (HALF, HALF), 1)
    masks[0] = jnp.where(row > lane, 0.0, NEG)
    masks[1] = jnp.where(row <= lane, 0.0, NEG)
    kpos = start - T + lax.broadcasted_iota(jnp.int32, (2 * T, 128), 0)
    flag[...] = ((kpos >= col_start) & (kpos < col_start + CB)).astype(jnp.float32)

    @pl.when(me == 0)
    def _():
        prev[...] = jnp.zeros_like(prev)

    @pl.when(me == n - 1)
    def _():
        back[...] = jnp.zeros_like(back)

    peers = S + len(dsteps)
    if relayed:

        @pl.when(middle)
        def _():
            pl.semaphore_wait(barrier, peers + 2)

        @pl.when((me != mid) & (me != mid - 1))
        def _():
            pl.semaphore_wait(barrier, peers + 1)

    else:

        @pl.when(has_other)
        def _():
            pl.semaphore_wait(barrier, peers + 1)

        @pl.when(ends)
        def _():
            pl.semaphore_wait(barrier, peers)

    def gather_step(s):
        return pltpu.make_async_remote_copy(
            src_ref=col,
            dst_ref=colr.at[s],
            send_sem=cg_s.at[s],
            recv_sem=cg_r.at[s],
            device_id={"ctx": flip(me, (steps + [1])[s])},
            device_id_type=MESH,
        )

    def halo(i, h):
        c = pl.ds(pl.multiple_of(h * D, D), D)
        return pltpu.make_async_remote_copy(
            src_ref=(k_ref, v_ref)[i].at[:, c],
            dst_ref=prev.at[i, :, c],
            send_sem=halo_s.at[i, h],
            recv_sem=halo_r.at[i, h],
            device_id={"ctx": me + 1},
            device_id_type=MESH,
        )

    def give_back(i, h):
        c = pl.ds(pl.multiple_of(h * D, D), D)
        return pltpu.make_async_remote_copy(
            src_ref=out.at[i, :, c],
            dst_ref=back.at[i, :, c],
            send_sem=ret_s.at[i, h],
            recv_sem=ret_r.at[i, h],
            device_id={"ctx": me - 1},
            device_id_type=MESH,
        )

    def reduce_step(s, h):
        return pltpu.make_async_remote_copy(
            src_ref=acc.at[h],
            dst_ref=accr.at[s, h],
            send_sem=red_s.at[s, h],
            recv_sem=red_r.at[s, h],
            device_id={"ctx": flip(me, (steps + [1])[s])},
            device_id_type=MESH,
        )

    def hop(i, h, first, source, target, to, send, recv):
        c = pl.ds(pl.multiple_of(h * D, D), D)
        return pltpu.make_async_remote_copy(
            src_ref=source.at[:, c] if first else source.at[i, :, c],
            dst_ref=target.at[i, :, c],
            send_sem=send.at[i, h],
            recv_sem=recv.at[i, h],
            device_id={"ctx": to},
            device_id_type=MESH,
        )

    def halo_out(i, h):
        return hop(i, h, True, (k_ref, v_ref)[i], relay, n - 1, halo_s, rel_r)

    def halo_on(i, h):
        return hop(i, h, False, relay, prev, mid, rel_s, halo_r)

    def back_out(i, h):
        return hop(i, h, False, out, relay, 0, ret_s, rel_r)

    def back_on(i, h):
        return hop(i, h, False, relay, back, mid - 1, rel_s, ret_r)

    def send_halo():
        round_about = (me == mid - 1) if relayed else (me < 0)

        @pl.when(me < n - 1)
        def _():
            @pl.loop(0, HEADS)
            def _(h):
                @pl.when(round_about & (h % 2 == 1))
                def _():
                    halo_out(0, h).start()
                    halo_out(1, h).start()

                @pl.when((me != mid - 1) | (h % 2 == 0) if relayed else (me >= 0))
                def _():
                    halo(0, h).start()
                    halo(1, h).start()

    send_halo()

    @pl.when(me % 2 == 1)
    def _():
        gather_step(0).start()
        gather_step(0).wait_send()
        gather_step(S).wait_recv()
        col[...] = colr[S]

    @pl.when(even)
    def _():
        gather_step(0).wait_recv()
        col[...] = col[...] + colr[0]
        for s in range(1, S):
            gather_step(s).start()
            gather_step(s).wait()
            col[...] = col[...] + colr[s]
        gather_step(S).start()

    def compute(h):
        @pl.when(me > 0)
        def _():
            halo(0, h).wait_recv()
            halo(1, h).wait_recv()

        c = pl.ds(pl.multiple_of(h * D, D), D)
        bias2 = bias_ref[pl.ds(h, 1), :] * LOG2E
        outside = jnp.where(me == 0, NEG, 0.0)
        kc = col[0:CB, c]
        vc = col[CB : 2 * CB, c]
        keys = [prev[0, 0:HALF, c], prev[0, HALF:T, c], k_ref[0:HALF, c], k_ref[HALF:T, c]]
        vals = [prev[1, 0:HALF, c], prev[1, HALF:T, c], v_ref[0:HALF, c], v_ref[HALF:T, c]]
        dks = [None] * 4
        dvs = [None] * 4
        dkc = dvc = None
        dbv = jnp.zeros((1, 128), jnp.float32)
        for b in range(2):
            rows = slice(b * HALF, (b + 1) * HALF)
            qb = q_ref[rows, c]
            gb = g_ref[rows, c]
            scores = []
            for p in range(3):
                j = b + p
                kb = flag[j * HALF : (j + 1) * HALF, :] * bias2
                if j < 2:
                    kb = kb + outside
                s = dot_nt(keys[j], qb) * (SCALE * LOG2E) + jnp.concatenate([kb, kb], axis=1)
                if p == 0:
                    s = s + masks[0]
                if p == 2:
                    s = s + masks[1]
                scores.append(s)
            cpos = col_start2 + lax.broadcasted_iota(jnp.int32, (CB, HALF), 0)
            qpos = start + b * HALF + lax.broadcasted_iota(jnp.int32, (CB, HALF), 1)
            sc = dot_nt(kc, qb) * (SCALE * LOG2E) + jnp.concatenate([bias2, bias2], axis=1)
            scores.append(jnp.where(cpos <= qpos - LOCAL_BAND, sc, NEG))
            top = functools.reduce(
                jnp.maximum, [jnp.max(s, axis=0, keepdims=True) for s in scores]
            )
            ps = [jnp.exp2(s - top) for s in scores]
            total = functools.reduce(jnp.add, [jnp.sum(p, axis=0, keepdims=True) for p in ps])
            inv = 1.0 / total
            ws = [p * inv for p in ps]
            w16 = [w.astype(jnp.bfloat16) for w in ws]
            vb = [vals[b], vals[b + 1], vals[b + 2], vc]
            kb = [keys[b], keys[b + 1], keys[b + 2], kc]
            ot = functools.reduce(jnp.add, [dot_tn(v, w) for v, w in zip(vb, w16)])
            ot = ot.astype(jnp.bfloat16).astype(jnp.float32)
            o_ref[rows, c] = ot.T.astype(jnp.bfloat16)
            delta = jnp.sum(gb.astype(jnp.float32).T * ot, axis=0, keepdims=True)
            ds = [w * (dot_nt(v, gb) - delta) for v, w in zip(vb, ws)]
            for p in range(3):
                j = b + p
                f = flag[j * HALF : (j + 1) * HALF, :]
                dbv = dbv + jnp.sum(fold(ds[p]) * f, axis=0, keepdims=True)
            dbv = dbv + jnp.sum(fold(ds[3]), axis=0, keepdims=True)
            ds16 = [d.astype(jnp.bfloat16) for d in ds]
            dqt = functools.reduce(jnp.add, [dot_tn(k, d) for k, d in zip(kb, ds16)])
            dq_ref[rows, c] = (dqt * SCALE).T.astype(jnp.bfloat16)
            for p in range(3):
                j = b + p
                dv = dot_nn(w16[p], gb)
                dk = dot_nn(ds16[p], qb)
                dvs[j] = dv if dvs[j] is None else dvs[j] + dv
                dks[j] = dk if dks[j] is None else dks[j] + dk
            dv = dot_nn(w16[3], gb)
            dk = dot_nn(ds16[3], qb)
            dvc = dv if dvc is None else dvc + dv
            dkc = dk if dkc is None else dkc + dk
        for j in range(2):
            rows = slice(j * HALF, (j + 1) * HALF)
            out[0, rows, c] = (dks[j] * SCALE).astype(jnp.bfloat16)
            out[1, rows, c] = dvs[j].astype(jnp.bfloat16)
            own[0, rows, c] = dks[j + 2] * SCALE
            own[1, rows, c] = dvs[j + 2]
        acc[h, 0:CB, :] = dkc * SCALE
        acc[h, CB : 2 * CB, :] = dvc
        acc[h, 2 * CB :, :] = jnp.broadcast_to(dbv, (8, 128))

        if relayed:

            @pl.when((me == mid) & (h % 2 == 0))
            def _():
                back_out(0, h).start()
                back_out(1, h).start()

        @pl.when((me > 0) & ((me != mid) | (h % 2 == 1)) if relayed else (me > 0))
        def _():
            give_back(0, h).start()
            give_back(1, h).start()

    def finish(h):
        @pl.when(me < n - 1)
        def _():
            give_back(0, h).wait_recv()
            give_back(1, h).wait_recv()

        c = pl.ds(pl.multiple_of(h * D, D), D)
        for i, ref in ((0, dk_ref), (1, dv_ref)):
            summed = acc[h, i * CB : (i + 1) * CB, :]
            for r in range(T // CB):
                rows = slice(r * CB, (r + 1) * CB)
                held = (col_start == start + r * CB).astype(jnp.float32)
                grad = own[i, rows, c] + back[i, rows, c].astype(jnp.float32) + summed * held
                ref[rows, c] = grad.astype(jnp.bfloat16)

    def turn(t, carry):
        @pl.when(t < HEADS)
        def _():
            compute(t)

        @pl.when(even & (t < HEADS))
        def _():
            reduce_step(0, t).start()

        for s in range(1, S + 1):
            h = t - s

            @pl.when((me % 2 == 1) & (h >= 0) & (h < HEADS))
            def _():
                if s == 1:
                    reduce_step(0, h).wait_recv()
                else:
                    reduce_step(s - 1, h).wait()
                acc[h] = acc[h] + accr[s - 1, h]
                reduce_step(s, h).start()
                if s == S:
                    finish(h)

        last = t - S - 1

        @pl.when(even & (last >= 0))
        def _():
            reduce_step(0, last).wait_send()
            reduce_step(S, last).wait_recv()
            acc[last] = accr[S, last]
            finish(last)

        if relayed:

            @pl.when((me == n - 1) & (t < HEADS // 2))
            def _():
                h = 2 * t + 1
                for i in range(2):
                    halo_out(i, h).wait_recv()
                    halo_on(i, h).start()

            @pl.when((me == 0) & (t >= 1) & (t <= HEADS) & (t % 2 == 1))
            def _():
                h = t - 1
                for i in range(2):
                    back_out(i, h).wait_recv()
                    back_on(i, h).start()

        return carry

    lax.fori_loop(0, HEADS + S + 1, turn, 0)

    for h in range(HEADS):
        bacc[h : h + 1, :] = acc[h, 2 * CB : 2 * CB + 1, :]
    for s in range(len(dsteps)):
        copy = pltpu.make_async_remote_copy(
            src_ref=bacc,
            dst_ref=baccr.at[s],
            send_sem=b_s.at[s],
            recv_sem=b_r.at[s],
            device_id={"dp": flip(mine, dsteps[s])},
            device_id_type=MESH,
        )
        copy.start()
        copy.wait()
        bacc[...] = bacc[...] + baccr[s]
    db_ref[...] = bacc[...]

    @pl.when(even)
    def _():
        gather_step(S).wait_send()

    @pl.when(me % 2 == 1)
    def _():
        @pl.loop(0, HEADS)
        def _(h):
            reduce_step(S, h).wait_send()

    if relayed:

        @pl.when(ends)
        def _():
            @pl.loop(0, HEADS // 2)
            def _(g):
                for i in range(2):
                    halo_on(i, 2 * g + me % 2).wait_send()

    @pl.when(me < n - 1)
    def _():
        @pl.loop(0, HEADS)
        def _(h):
            halo(0, h).wait_send()
            halo(1, h).wait_send()

    @pl.when(me > 0)
    def _():
        @pl.loop(0, HEADS)
        def _(h):
            give_back(0, h).wait_send()
            give_back(1, h).wait_send()


def per_device(queries, key_vectors, value_vectors, out_grad, column_bias, column_offsets):
    if column_offsets.shape[0] > 1:
        return per_device_many_windows(
            queries, key_vectors, value_vectors, out_grad, column_bias, column_offsets
        )
    n = lax.axis_size("ctx")
    ndp = lax.axis_size("dp")
    S = n.bit_length() - 1
    SD = ndp.bit_length() - 1
    width = queries.shape[2]
    vmem = pl.BlockSpec(memory_space=pltpu.VMEM)
    wide = jax.ShapeDtypeStruct((T, width), jnp.bfloat16)
    o, dq, dk, dv, db = pl.pallas_call(
        functools.partial(fused_kernel, n, ndp),
        out_shape=(wide, wide, wide, wide, jax.ShapeDtypeStruct((HEADS, 128), jnp.float32)),
        in_specs=[vmem, vmem, vmem, vmem, vmem, vmem],
        out_specs=(vmem, vmem, vmem, vmem, vmem),
        scratch_shapes=[
            pltpu.VMEM((2, T, width), jnp.bfloat16),
            pltpu.VMEM((2, T, width), jnp.bfloat16),
            pltpu.VMEM((2, T, width), jnp.bfloat16),
            pltpu.VMEM((2, T, width), jnp.float32),
            pltpu.VMEM((2 * CB, width), jnp.bfloat16),
            pltpu.VMEM((S + 1, 2 * CB, width), jnp.bfloat16),
            pltpu.VMEM((HEADS, 2 * CB + 8, 128), jnp.float32),
            pltpu.VMEM((S + 1, HEADS, 2 * CB + 8, 128), jnp.float32),
            pltpu.VMEM((HEADS, 128), jnp.float32),
            pltpu.VMEM((SD, HEADS, 128), jnp.float32),
            pltpu.VMEM((2 * T, 128), jnp.float32),
            pltpu.VMEM((2, HALF, HALF), jnp.float32),
            pltpu.VMEM((2, T, width), jnp.bfloat16),
            pltpu.SemaphoreType.DMA((2, HEADS)),
            pltpu.SemaphoreType.DMA((2, HEADS)),
            pltpu.SemaphoreType.DMA((2, HEADS)),
            pltpu.SemaphoreType.DMA((2, HEADS)),
            pltpu.SemaphoreType.DMA((2, HEADS)),
            pltpu.SemaphoreType.DMA((2, HEADS)),
            pltpu.SemaphoreType.DMA((S + 1,)),
            pltpu.SemaphoreType.DMA((S + 1,)),
            pltpu.SemaphoreType.DMA((S + 1, HEADS)),
            pltpu.SemaphoreType.DMA((S + 1, HEADS)),
            pltpu.SemaphoreType.DMA((SD,)),
            pltpu.SemaphoreType.DMA((SD,)),
        ],
        compiler_params=pltpu.CompilerParams(
            collective_id=0, has_side_effects=True, vmem_limit_bytes=56 * 2**20
        ),
    )(
        jnp.broadcast_to(column_offsets[:, None] * CB, (8, width)),
        jnp.broadcast_to(column_bias[:, None], (HEADS, 128)),
        queries[0],
        key_vectors[0],
        value_vectors[0],
        out_grad[0],
    )
    return o[None], dq[None], dk[None], dv[None], jnp.sum(db, axis=1)


def solution(mesh):
    placed = (
        P("dp", "ctx", None),
        P("dp", "ctx", None),
        P("dp", "ctx", None),
        P("dp", "ctx", None),
        P(),
        P(),
    )
    return jax.shard_map(
        per_device,
        mesh=mesh,
        in_specs=placed,
        out_specs=(
            P("dp", "ctx", None),
            P("dp", "ctx", None),
            P("dp", "ctx", None),
            P("dp", "ctx", None),
            P(),
        ),
        check_vma=False,
    )
```

```python
import functools

import jax
import jax.numpy as jnp
from jax import lax
from jax.experimental import pallas as pl
from jax.experimental.pallas import tpu as pltpu
from jax.sharding import PartitionSpec as P

HEADS = 8
HEAD_DIM = 128
LOCAL_BAND = 512
STRIDE = 4096
CB = 64
TOKENS_PER_SHARD = 512


def from_behind(value, axis, by):
    size = lax.axis_size(axis)
    pairs = [(i, i + by) for i in range(size) if 0 <= i + by < size]
    return lax.ppermute(value, axis, pairs)


def column_flags(positions, offsets):
    window = positions // STRIDE
    within = positions % STRIDE
    picks = window[:, None] == jnp.arange(offsets.shape[0], dtype=jnp.int32)[None, :]
    offset_at = jnp.sum(jnp.where(picks, offsets[None, :], 0), axis=1)
    return (positions >= 0) & (within // CB == offset_at)


def head_block(qh, kb, vb, kc, vc, doh, bias_h, band_ok, band_col, col_ok):
    scale = HEAD_DIM ** (-0.5)
    sb = (
        jnp.dot(qh, kb.T, preferred_element_type=jnp.float32) * scale
        + jnp.where(band_col, bias_h, 0.0)[None, :]
    )
    sc = jnp.dot(qh, kc.T, preferred_element_type=jnp.float32) * scale + bias_h
    sb = jnp.where(band_ok, sb, -jnp.inf)
    sc = jnp.where(col_ok, sc, -jnp.inf)
    top = jnp.maximum(jnp.max(sb, axis=1), jnp.max(sc, axis=1))
    pb = jnp.exp(sb - top[:, None])
    pc = jnp.exp(sc - top[:, None])
    total = jnp.sum(pb, axis=1) + jnp.sum(pc, axis=1)
    wb = pb / total[:, None]
    wc = pc / total[:, None]
    wb16 = wb.astype(jnp.bfloat16)
    wc16 = wc.astype(jnp.bfloat16)
    mixed = jnp.dot(wb16, vb, preferred_element_type=jnp.float32) + jnp.dot(
        wc16, vc, preferred_element_type=jnp.float32
    )
    oh = mixed.astype(jnp.bfloat16)
    delta = jnp.sum(doh.astype(jnp.float32) * oh.astype(jnp.float32), axis=1)
    dsb = wb * (jnp.dot(doh, vb.T, preferred_element_type=jnp.float32) - delta[:, None])
    dsc = wc * (jnp.dot(doh, vc.T, preferred_element_type=jnp.float32) - delta[:, None])
    dbias = jnp.sum(jnp.where(band_col[None, :], dsb, 0.0)) + jnp.sum(dsc)
    dsb16 = dsb.astype(jnp.bfloat16)
    dsc16 = dsc.astype(jnp.bfloat16)
    dq = (
        (
            jnp.dot(dsb16, kb, preferred_element_type=jnp.float32)
            + jnp.dot(dsc16, kc, preferred_element_type=jnp.float32)
        )
        * scale
    ).astype(jnp.bfloat16)
    dkb = jnp.dot(dsb16.T, qh, preferred_element_type=jnp.float32) * scale
    dvb = jnp.dot(wb16.T, doh, preferred_element_type=jnp.float32)
    dkc = jnp.dot(dsc16.T, qh, preferred_element_type=jnp.float32) * scale
    dvc = jnp.dot(wc16.T, doh, preferred_element_type=jnp.float32)
    return (oh, dq, dkb, dvb, dkc, dvc, dbias, top, total, delta)


def separate_heads(x):
    return x.reshape(x.shape[0], HEADS, HEAD_DIM).transpose(1, 0, 2)


def join_heads(x):
    return x.transpose(1, 0, 2).reshape(x.shape[1], HEADS * HEAD_DIM)


def per_device_many_windows(queries, key_vectors, value_vectors, out_grad, column_bias, column_offsets):
    here = lax.axis_index("ctx")
    count = lax.axis_size("ctx")
    start_position = here * TOKENS_PER_SHARD
    width = queries.shape[2]
    query_rows = queries[0]
    key_rows = key_vectors[0]
    value_rows = value_vectors[0]
    grad_rows = out_grad[0]
    ncol = column_offsets.shape[0]
    block_starts = jnp.arange(ncol, dtype=jnp.int32) * STRIDE + column_offsets * CB
    colpos = jnp.repeat(block_starts, CB) + jnp.tile(jnp.arange(CB, dtype=jnp.int32), ncol)
    window = start_position // STRIDE
    own_start = window * STRIDE + column_offsets[window] * CB
    local = jnp.clip(own_start - start_position, 0, TOKENS_PER_SHARD - CB)
    piece_k = lax.dynamic_slice_in_dim(key_rows, local, CB, 0)
    piece_v = lax.dynamic_slice_in_dim(value_rows, local, CB, 0)
    pieces_k, pieces_v = (
        lax.all_gather(piece_k, "ctx", axis=0, tiled=True),
        lax.all_gather(piece_v, "ctx", axis=0, tiled=True),
    )
    owner = block_starts // TOKENS_PER_SHARD
    col_k = pieces_k.reshape(count, CB, width)[owner].reshape(ncol * CB, width)
    col_v = pieces_v.reshape(count, CB, width)[owner].reshape(ncol * CB, width)
    prev_k, prev_v = from_behind((key_rows, value_rows), "ctx", 1)
    band_k = jnp.concatenate([prev_k, key_rows], axis=0)
    band_v = jnp.concatenate([prev_v, value_rows], axis=0)
    qpos = start_position + jnp.arange(TOKENS_PER_SHARD, dtype=jnp.int32)
    kpos = start_position - LOCAL_BAND + jnp.arange(LOCAL_BAND + TOKENS_PER_SHARD, dtype=jnp.int32)
    gap = qpos[:, None] - kpos[None, :]
    band_ok = (kpos[None, :] >= 0) & (gap >= 0) & (gap < LOCAL_BAND)
    band_col = column_flags(kpos, column_offsets)
    col_ok = colpos[None, :] <= qpos[:, None] - LOCAL_BAND

    def per_head(items):
        return head_block(
            items[0],
            items[1],
            items[2],
            items[3],
            items[4],
            items[5],
            items[6],
            band_ok,
            band_col,
            col_ok,
        )

    results = lax.map(
        per_head,
        (
            separate_heads(query_rows),
            separate_heads(band_k),
            separate_heads(band_v),
            separate_heads(col_k),
            separate_heads(col_v),
            separate_heads(grad_rows),
            column_bias,
        ),
    )
    oh, dq, dkb, dvb, dkc, dvc, dbias, top, total, delta = results
    attended = join_heads(oh)
    query_grad = join_heads(dq)
    dk_band = join_heads(dkb)
    dv_band = join_heads(dvb)
    own_dk = dk_band[dk_band.shape[0] - TOKENS_PER_SHARD :]
    own_dv = dv_band[dv_band.shape[0] - TOKENS_PER_SHARD :]
    back_k, back_v = from_behind((dk_band[:LOCAL_BAND], dv_band[:LOCAL_BAND]), "ctx", -1)
    own_dk = own_dk.at[TOKENS_PER_SHARD - LOCAL_BAND :].add(back_k)
    own_dv = own_dv.at[TOKENS_PER_SHARD - LOCAL_BAND :].add(back_v)
    summed_k, summed_v = lax.psum((join_heads(dkc), join_heads(dvc)), "ctx")
    flags = column_flags(qpos, column_offsets)
    source = jnp.clip(qpos // STRIDE * CB + qpos % CB, 0, ncol * CB - 1)
    own_dk = own_dk + jnp.where(flags[:, None], summed_k[source], 0.0)
    own_dv = own_dv + jnp.where(flags[:, None], summed_v[source], 0.0)
    bias_grad = lax.psum(dbias, ("dp", "ctx"))
    return (
        attended[None],
        query_grad[None],
        own_dk.astype(jnp.bfloat16)[None],
        own_dv.astype(jnp.bfloat16)[None],
        bias_grad,
    )


LOG2E = 1.4426950408889634
SCALE = HEAD_DIM ** (-0.5)
NEG = -1e30
HALF = 256
T = TOKENS_PER_SHARD
D = HEAD_DIM
MESH = pl.DeviceIdType.MESH
NT = (((1,), (1,)), ((), ()))
TN = (((0,), (0,)), ((), ()))


def dot_nt(a, b):
    return lax.dot_general(a, b, NT, preferred_element_type=jnp.float32)


def dot_tn(a, b):
    return lax.dot_general(a, b, TN, preferred_element_type=jnp.float32)


def dot_nn(a, b):
    return jnp.dot(a, b, preferred_element_type=jnp.float32)


def flip(index, step):
    return index + step * (1 - 2 * ((index // step) % 2))


def fold(x):
    return x[:, :128] + x[:, 128:]


def fused_kernel(
    n,
    ndp,
    offs_ref,
    bias_ref,
    q_ref,
    k_ref,
    v_ref,
    g_ref,
    o_ref,
    dq_ref,
    dk_ref,
    dv_ref,
    db_ref,
    prev,
    back,
    out,
    own,
    col,
    colr,
    acc,
    accr,
    bacc,
    baccr,
    flag,
    masks,
    relay,
    rel_s,
    rel_r,
    halo_s,
    halo_r,
    ret_s,
    ret_r,
    cg_s,
    cg_r,
    red_s,
    red_r,
    b_s,
    b_r,
):
    me = lax.axis_index("ctx")
    mine = lax.axis_index("dp")
    steps = []
    while 2 ** len(steps) < n:
        steps.append(2 ** len(steps))
    dsteps = []
    while 2 ** len(dsteps) < ndp:
        dsteps.append(2 ** len(dsteps))
    S = len(steps)
    start = me * T
    col_row = offs_ref[0:1, :]
    col_start = col_row[:, 0:128]
    col_start2 = col_row[:, 0:HALF]

    even = me % 2 == 0
    mid = n // 2
    relayed = False
    other = me + 2 * (me % 2) - 1
    has_other = (other >= 0) & (other < n)
    ends = (me == 0) | (me == n - 1)
    middle = (me == mid - 1) | (me == mid)
    barrier = pltpu.get_barrier_semaphore()
    for st in steps:
        pl.semaphore_signal(barrier, inc=1, device_id={"ctx": flip(me, st)}, device_id_type=MESH)
    for st in dsteps:
        pl.semaphore_signal(barrier, inc=1, device_id={"dp": flip(mine, st)}, device_id_type=MESH)

    @pl.when(has_other)
    def _():
        pl.semaphore_signal(barrier, inc=1, device_id={"ctx": other}, device_id_type=MESH)

    if relayed:

        @pl.when(ends | middle)
        def _():
            pl.semaphore_signal(barrier, inc=1, device_id={"ctx": flip(flip(me, 1), 2)}, device_id_type=MESH)

    for i, ref in ((0, k_ref), (1, v_ref)):
        block = jnp.zeros((CB, ref.shape[1]), jnp.float32)
        for r in range(T // CB):
            held = (col_row == start + r * CB).astype(jnp.float32)
            block = block + ref[r * CB : (r + 1) * CB, :].astype(jnp.float32) * held
        col[i * CB : (i + 1) * CB, :] = block.astype(jnp.bfloat16)

    row = lax.broadcasted_iota(jnp.int32, (HALF, HALF), 0)
    lane = lax.broadcasted_iota(jnp.int32, (HALF, HALF), 1)
    masks[0] = jnp.where(row > lane, 0.0, NEG)
    masks[1] = jnp.where(row <= lane, 0.0, NEG)
    kpos = start - T + lax.broadcasted_iota(jnp.int32, (2 * T, 128), 0)
    flag[...] = ((kpos >= col_start) & (kpos < col_start + CB)).astype(jnp.float32)

    @pl.when(me == 0)
    def _():
        prev[...] = jnp.zeros_like(prev)

    @pl.when(me == n - 1)
    def _():
        back[...] = jnp.zeros_like(back)

    peers = S + len(dsteps)
    if relayed:

        @pl.when(middle)
        def _():
            pl.semaphore_wait(barrier, peers + 2)

        @pl.when((me != mid) & (me != mid - 1))
        def _():
            pl.semaphore_wait(barrier, peers + 1)

    else:

        @pl.when(has_other)
        def _():
            pl.semaphore_wait(barrier, peers + 1)

        @pl.when(ends)
        def _():
            pl.semaphore_wait(barrier, peers)

    def gather_step(s):
        return pltpu.make_async_remote_copy(
            src_ref=col,
            dst_ref=colr.at[s],
            send_sem=cg_s.at[s],
            recv_sem=cg_r.at[s],
            device_id={"ctx": flip(me, (steps + [1])[s])},
            device_id_type=MESH,
        )

    def halo(i, h):
        c = pl.ds(pl.multiple_of(h * D, D), D)
        return pltpu.make_async_remote_copy(
            src_ref=(k_ref, v_ref)[i].at[:, c],
            dst_ref=prev.at[i, :, c],
            send_sem=halo_s.at[i, h],
            recv_sem=halo_r.at[i, h],
            device_id={"ctx": me + 1},
            device_id_type=MESH,
        )

    def give_back(i, h):
        c = pl.ds(pl.multiple_of(h * D, D), D)
        return pltpu.make_async_remote_copy(
            src_ref=out.at[i, :, c],
            dst_ref=back.at[i, :, c],
            send_sem=ret_s.at[i, h],
            recv_sem=ret_r.at[i, h],
            device_id={"ctx": me - 1},
            device_id_type=MESH,
        )

    def reduce_step(s, h):
        return pltpu.make_async_remote_copy(
            src_ref=acc.at[h],
            dst_ref=accr.at[s, h],
            send_sem=red_s.at[s, h],
            recv_sem=red_r.at[s, h],
            device_id={"ctx": flip(me, (steps + [1])[s])},
            device_id_type=MESH,
        )

    def hop(i, h, first, source, target, to, send, recv):
        c = pl.ds(pl.multiple_of(h * D, D), D)
        return pltpu.make_async_remote_copy(
            src_ref=source.at[:, c] if first else source.at[i, :, c],
            dst_ref=target.at[i, :, c],
            send_sem=send.at[i, h],
            recv_sem=recv.at[i, h],
            device_id={"ctx": to},
            device_id_type=MESH,
        )

    def halo_out(i, h):
        return hop(i, h, True, (k_ref, v_ref)[i], relay, n - 1, halo_s, rel_r)

    def halo_on(i, h):
        return hop(i, h, False, relay, prev, mid, rel_s, halo_r)

    def back_out(i, h):
        return hop(i, h, False, out, relay, 0, ret_s, rel_r)

    def back_on(i, h):
        return hop(i, h, False, relay, back, mid - 1, rel_s, ret_r)

    def send_halo():
        round_about = (me == mid - 1) if relayed else (me < 0)

        @pl.when(me < n - 1)
        def _():
            @pl.loop(0, HEADS)
            def _(h):
                @pl.when(round_about & (h % 2 == 1))
                def _():
                    halo_out(0, h).start()
                    halo_out(1, h).start()

                @pl.when((me != mid - 1) | (h % 2 == 0) if relayed else (me >= 0))
                def _():
                    halo(0, h).start()
                    halo(1, h).start()

    send_halo()

    @pl.when(me % 2 == 1)
    def _():
        gather_step(0).start()
        gather_step(0).wait_send()
        gather_step(S).wait_recv()
        col[...] = colr[S]

    @pl.when(even)
    def _():
        gather_step(0).wait_recv()
        col[...] = col[...] + colr[0]
        for s in range(1, S):
            gather_step(s).start()
            gather_step(s).wait()
            col[...] = col[...] + colr[s]
        gather_step(S).start()

    def compute(h):
        @pl.when(me > 0)
        def _():
            halo(0, h).wait_recv()
            halo(1, h).wait_recv()

        c = pl.ds(pl.multiple_of(h * D, D), D)
        bias2 = bias_ref[pl.ds(h, 1), :] * LOG2E
        outside = jnp.where(me == 0, NEG, 0.0)
        kc = col[0:CB, c]
        vc = col[CB : 2 * CB, c]
        keys = [prev[0, 0:HALF, c], prev[0, HALF:T, c], k_ref[0:HALF, c], k_ref[HALF:T, c]]
        vals = [prev[1, 0:HALF, c], prev[1, HALF:T, c], v_ref[0:HALF, c], v_ref[HALF:T, c]]
        dks = [None] * 4
        dvs = [None] * 4
        dkc = dvc = None
        dbv = jnp.zeros((1, 128), jnp.float32)
        for b in range(2):
            rows = slice(b * HALF, (b + 1) * HALF)
            qb = q_ref[rows, c]
            gb = g_ref[rows, c]
            scores = []
            for p in range(3):
                j = b + p
                kb = flag[j * HALF : (j + 1) * HALF, :] * bias2
                if j < 2:
                    kb = kb + outside
                s = dot_nt(keys[j], qb) * (SCALE * LOG2E) + jnp.concatenate([kb, kb], axis=1)
                if p == 0:
                    s = s + masks[0]
                if p == 2:
                    s = s + masks[1]
                scores.append(s)
            cpos = col_start2 + lax.broadcasted_iota(jnp.int32, (CB, HALF), 0)
            qpos = start + b * HALF + lax.broadcasted_iota(jnp.int32, (CB, HALF), 1)
            sc = dot_nt(kc, qb) * (SCALE * LOG2E) + jnp.concatenate([bias2, bias2], axis=1)
            scores.append(jnp.where(cpos <= qpos - LOCAL_BAND, sc, NEG))
            top = functools.reduce(
                jnp.maximum, [jnp.max(s, axis=0, keepdims=True) for s in scores]
            )
            ps = [jnp.exp2(s - top) for s in scores]
            total = functools.reduce(jnp.add, [jnp.sum(p, axis=0, keepdims=True) for p in ps])
            inv = 1.0 / total
            ws = [p * inv for p in ps]
            w16 = [w.astype(jnp.bfloat16) for w in ws]
            vb = [vals[b], vals[b + 1], vals[b + 2], vc]
            kb = [keys[b], keys[b + 1], keys[b + 2], kc]
            ot = functools.reduce(jnp.add, [dot_tn(v, w) for v, w in zip(vb, w16)])
            ot = ot.astype(jnp.bfloat16).astype(jnp.float32)
            o_ref[rows, c] = ot.T.astype(jnp.bfloat16)
            delta = jnp.sum(gb.astype(jnp.float32).T * ot, axis=0, keepdims=True)
            ds = [w * (dot_nt(v, gb) - delta) for v, w in zip(vb, ws)]
            for p in range(3):
                j = b + p
                f = flag[j * HALF : (j + 1) * HALF, :]
                dbv = dbv + jnp.sum(fold(ds[p]) * f, axis=0, keepdims=True)
            dbv = dbv + jnp.sum(fold(ds[3]), axis=0, keepdims=True)
            ds16 = [d.astype(jnp.bfloat16) for d in ds]
            dqt = functools.reduce(jnp.add, [dot_tn(k, d) for k, d in zip(kb, ds16)])
            dq_ref[rows, c] = (dqt * SCALE).T.astype(jnp.bfloat16)
            for p in range(3):
                j = b + p
                dv = dot_nn(w16[p], gb)
                dk = dot_nn(ds16[p], qb)
                dvs[j] = dv if dvs[j] is None else dvs[j] + dv
                dks[j] = dk if dks[j] is None else dks[j] + dk
            dv = dot_nn(w16[3], gb)
            dk = dot_nn(ds16[3], qb)
            dvc = dv if dvc is None else dvc + dv
            dkc = dk if dkc is None else dkc + dk
        for j in range(2):
            rows = slice(j * HALF, (j + 1) * HALF)
            out[0, rows, c] = (dks[j] * SCALE).astype(jnp.bfloat16)
            out[1, rows, c] = dvs[j].astype(jnp.bfloat16)
            own[0, rows, c] = dks[j + 2] * SCALE
            own[1, rows, c] = dvs[j + 2]
        acc[h, 0:CB, :] = dkc * SCALE
        acc[h, CB : 2 * CB, :] = dvc
        acc[h, 2 * CB :, :] = jnp.broadcast_to(dbv, (8, 128))

        if relayed:

            @pl.when((me == mid) & (h % 2 == 0))
            def _():
                back_out(0, h).start()
                back_out(1, h).start()

        @pl.when((me > 0) & ((me != mid) | (h % 2 == 1)) if relayed else (me > 0))
        def _():
            give_back(0, h).start()
            give_back(1, h).start()

    def finish(h):
        @pl.when(me < n - 1)
        def _():
            give_back(0, h).wait_recv()
            give_back(1, h).wait_recv()

        c = pl.ds(pl.multiple_of(h * D, D), D)
        for i, ref in ((0, dk_ref), (1, dv_ref)):
            summed = acc[h, i * CB : (i + 1) * CB, :]
            for r in range(T // CB):
                rows = slice(r * CB, (r + 1) * CB)
                held = (col_start == start + r * CB).astype(jnp.float32)
                grad = own[i, rows, c] + back[i, rows, c].astype(jnp.float32) + summed * held
                ref[rows, c] = grad.astype(jnp.bfloat16)

    def turn(t, carry):
        @pl.when(t < HEADS)
        def _():
            compute(t)

        @pl.when(even & (t < HEADS))
        def _():
            reduce_step(0, t).start()

        for s in range(1, S + 1):
            h = t - s

            @pl.when((me % 2 == 1) & (h >= 0) & (h < HEADS))
            def _():
                if s == 1:
                    reduce_step(0, h).wait_recv()
                else:
                    reduce_step(s - 1, h).wait()
                acc[h] = acc[h] + accr[s - 1, h]
                reduce_step(s, h).start()
                if s == S:
                    finish(h)

        last = t - S - 1

        @pl.when(even & (last >= 0))
        def _():
            reduce_step(0, last).wait_send()
            reduce_step(S, last).wait_recv()
            acc[last] = accr[S, last]
            finish(last)

        if relayed:

            @pl.when((me == n - 1) & (t < HEADS // 2))
            def _():
                h = 2 * t + 1
                for i in range(2):
                    halo_out(i, h).wait_recv()
                    halo_on(i, h).start()

            @pl.when((me == 0) & (t >= 1) & (t <= HEADS) & (t % 2 == 1))
            def _():
                h = t - 1
                for i in range(2):
                    back_out(i, h).wait_recv()
                    back_on(i, h).start()

        return carry

    lax.fori_loop(0, HEADS + S + 1, turn, 0)

    for h in range(HEADS):
        bacc[h : h + 1, :] = acc[h, 2 * CB : 2 * CB + 1, :]
    for s in range(len(dsteps)):
        copy = pltpu.make_async_remote_copy(
            src_ref=bacc,
            dst_ref=baccr.at[s],
            send_sem=b_s.at[s],
            recv_sem=b_r.at[s],
            device_id={"dp": flip(mine, dsteps[s])},
            device_id_type=MESH,
        )
        copy.start()
        copy.wait()
        bacc[...] = bacc[...] + baccr[s]
    db_ref[...] = bacc[...]

    @pl.when(even)
    def _():
        gather_step(S).wait_send()

    @pl.when(me % 2 == 1)
    def _():
        @pl.loop(0, HEADS)
        def _(h):
            reduce_step(S, h).wait_send()

    if relayed:

        @pl.when(ends)
        def _():
            @pl.loop(0, HEADS // 2)
            def _(g):
                for i in range(2):
                    halo_on(i, 2 * g + me % 2).wait_send()

    @pl.when(me < n - 1)
    def _():
        @pl.loop(0, HEADS)
        def _(h):
            halo(0, h).wait_send()
            halo(1, h).wait_send()

    @pl.when(me > 0)
    def _():
        @pl.loop(0, HEADS)
        def _(h):
            give_back(0, h).wait_send()
            give_back(1, h).wait_send()


def per_device(queries, key_vectors, value_vectors, out_grad, column_bias, column_offsets):
    if column_offsets.shape[0] > 1:
        return per_device_many_windows(
            queries, key_vectors, value_vectors, out_grad, column_bias, column_offsets
        )
    n = lax.axis_size("ctx")
    ndp = lax.axis_size("dp")
    S = n.bit_length() - 1
    SD = ndp.bit_length() - 1
    width = queries.shape[2]
    vmem = pl.BlockSpec(memory_space=pltpu.VMEM)
    wide = jax.ShapeDtypeStruct((T, width), jnp.bfloat16)
    o, dq, dk, dv, db = pl.pallas_call(
        functools.partial(fused_kernel, n, ndp),
        out_shape=(wide, wide, wide, wide, jax.ShapeDtypeStruct((HEADS, 128), jnp.float32)),
        in_specs=[vmem, vmem, vmem, vmem, vmem, vmem],
        out_specs=(vmem, vmem, vmem, vmem, vmem),
        scratch_shapes=[
            pltpu.VMEM((2, T, width), jnp.bfloat16),
            pltpu.VMEM((2, T, width), jnp.bfloat16),
            pltpu.VMEM((2, T, width), jnp.bfloat16),
            pltpu.VMEM((2, T, width), jnp.float32),
            pltpu.VMEM((2 * CB, width), jnp.bfloat16),
            pltpu.VMEM((S + 1, 2 * CB, width), jnp.bfloat16),
            pltpu.VMEM((HEADS, 2 * CB + 8, 128), jnp.float32),
            pltpu.VMEM((S + 1, HEADS, 2 * CB + 8, 128), jnp.float32),
            pltpu.VMEM((HEADS, 128), jnp.float32),
            pltpu.VMEM((SD, HEADS, 128), jnp.float32),
            pltpu.VMEM((2 * T, 128), jnp.float32),
            pltpu.VMEM((2, HALF, HALF), jnp.float32),
            pltpu.VMEM((2, T, width), jnp.bfloat16),
            pltpu.SemaphoreType.DMA((2, HEADS)),
            pltpu.SemaphoreType.DMA((2, HEADS)),
            pltpu.SemaphoreType.DMA((2, HEADS)),
            pltpu.SemaphoreType.DMA((2, HEADS)),
            pltpu.SemaphoreType.DMA((2, HEADS)),
            pltpu.SemaphoreType.DMA((2, HEADS)),
            pltpu.SemaphoreType.DMA((S + 1,)),
            pltpu.SemaphoreType.DMA((S + 1,)),
            pltpu.SemaphoreType.DMA((S + 1, HEADS)),
            pltpu.SemaphoreType.DMA((S + 1, HEADS)),
            pltpu.SemaphoreType.DMA((SD,)),
            pltpu.SemaphoreType.DMA((SD,)),
        ],
        compiler_params=pltpu.CompilerParams(
            collective_id=0, has_side_effects=True, vmem_limit_bytes=56 * 2**20
        ),
    )(
        jnp.broadcast_to(column_offsets[:, None] * CB, (8, width)),
        jnp.broadcast_to(column_bias[:, None], (HEADS, 128)),
        queries[0],
        key_vectors[0],
        value_vectors[0],
        out_grad[0],
    )
    return o[None], dq[None], dk[None], dv[None], jnp.sum(db, axis=1)


def solution(mesh):
    placed = (
        P("dp", "ctx", None),
        P("dp", "ctx", None),
        P("dp", "ctx", None),
        P("dp", "ctx", None),
        P(),
        P(),
    )
    return jax.shard_map(
        per_device,
        mesh=mesh,
        in_specs=placed,
        out_specs=(
            P("dp", "ctx", None),
            P("dp", "ctx", None),
            P("dp", "ctx", None),
            P("dp", "ctx", None),
            P(),
        ),
        check_vma=False,
    )
```
